32 devices in a mesh: dp: 4 (over x, core), row: 4 (over z), col: 2 (over y).
Axes of the slice: x: 2, y: 2, z: 4, core: 2. Of those that a mesh axis runs over, the one named last changes fastest.
Arguments:
- tokens_in: bfloat16 [8192, 768], P(('dp', 'col'), 'row'), may hold values from -6 to 6
- out_cot: bfloat16 [8192, 768], P(('dp', 'col'), 'row'), may hold values from -6 to 6
- segments: int32 [16, 512], P('dp'), may hold values from 0 to 31, never falling along the last dimension, each value on 1 to 256 neighbouring positions
- norm_params: float32 [4, 768], P(None, 'row'), may hold values from -1.2 to 1.5, as said below
- qkv_weight: float32 [768, 2304], P('row', 'col'), may hold values from -0.21875 to 0.21875
- proj_weight: float32 [768, 768], P('col', 'row'), may hold values from -0.875 to 0.875
- up_weight: float32 [768, 3072], P('row', 'col'), may hold values from -0.21875 to 0.21875
- down_weight: float32 [3072, 768], P('col', 'row'), may hold values from -0.109375 to 0.109375
- norm_first: float32 [4, 768], P(None, 'row'), may hold values from -18 to 18
- norm_second: float32 [4, 768], P(None, 'row'), may hold values from 30 to 300
- qkv_first: float32 [768, 2304], P('row', 'col'), may hold values from -18 to 18
- qkv_second: float32 [768, 2304], P('row', 'col'), may hold values from 30 to 300
- proj_first: float32 [768, 768], P('col', 'row'), may hold values from -18 to 18
- proj_second: float32 [768, 768], P('col', 'row'), may hold values from 30 to 300
- up_first: float32 [768, 3072], P('row', 'col'), may hold values from -18 to 18
- up_second: float32 [768, 3072], P('row', 'col'), may hold values from 30 to 300
- down_first: float32 [3072, 768], P('col', 'row'), may hold values from -18 to 18
- down_second: float32 [3072, 768], P('col', 'row'), may hold values from 30 to 300
Outputs:
- output: bfloat16 [8192, 768], P(('dp', 'col'), 'row')
- input_grad: bfloat16 [8192, 768], P(('dp', 'col'), 'row')
- norm_grad: float32 [4, 768], P(None, 'row')
- qkv_grad: float32 [768, 2304], P('row', 'col')
- proj_grad: float32 [768, 768], P('col', 'row')
- up_grad: float32 [768, 3072], P('row', 'col')
- down_grad: float32 [3072, 768], P('col', 'row')
- norm_new: float32 [4, 768], P(None, 'row')
- qkv_new: float32 [768, 2304], P('row', 'col')
- proj_new: float32 [768, 768], P('col', 'row')
- up_new: float32 [768, 3072], P('row', 'col')
- down_new: float32 [3072, 768], P('col', 'row')
- norm_first_new: float32 [4, 768], P(None, 'row')
- norm_second_new: float32 [4, 768], P(None, 'row')
- qkv_first_new: float32 [768, 2304], P('row', 'col')
- qkv_second_new: float32 [768, 2304], P('row', 'col')
- proj_first_new: float32 [768, 768], P('col', 'row')
- proj_second_new: float32 [768, 768], P('col', 'row')
- up_first_new: float32 [768, 3072], P('row', 'col')
- up_second_new: float32 [768, 3072], P('row', 'col')
- down_first_new: float32 [3072, 768], P('col', 'row')
- down_second_new: float32 [3072, 768], P('col', 'row')
The draws below stay inside these ranges and needn't reach their ends.
Inputs may be any that keep to these rules, and one draw needn't show every extreme that they name: `segments`: within a row the numbers never fall; no number covers more than 256 positions of a row, and one covers exactly that many. `norm_params`: rows 0 and 2 lie in 0.5 to 1.5.
All inputs are finite; a program needn't handle non-finite values.
Results may differ from the reference program's by a relative error of at most 0.0093.
Values may be sent and summed in bfloat16 or wider, within the bound.
A program may use at most 192 MiB of HBM per device.

```python
import math
import jax
import jax.numpy as jnp
import numpy as np
from jax import lax

D = 768
HEADS = 12
HEAD_DIM = 64
ROT_DIM = 16
FF = 3072
SEQ_LEN = 512
STEP = 3
SEQUENCES = 16
TOKENS = 8192


def draw_norm_params(key, part):
    gain_key, bias_key = jax.random.split(key)
    gains = jax.random.uniform(gain_key, (2, D), jnp.float32, 0.5, 1.5)
    biases = jnp.clip(0.3 * jax.random.normal(bias_key, (2, D), jnp.float32), -1.2, 1.2)
    return jnp.stack([gains[0], biases[0], gains[1], biases[1]], 0)


def levels(stream_key, shape, cuts, least, high):
    gain = 1.0
    for dim, parts in cuts:
        draws = jax.random.uniform(jax.random.fold_in(jax.random.fold_in(stream_key, 6), dim), (parts,), jnp.float32, least / len(cuts), high / len(cuts))
        gain = gain * jnp.repeat(jnp.exp(draws), shape[dim] // parts).reshape((-1,) + (1,) * (len(shape) - 1 - dim))
    return gain


def profile(count, total, most, slope):
    portions = [(1 << 20) // math.isqrt(standing ** slope) + 1 for standing in range(2, count + 1)]
    surplus, holding = total - most - (count - 1), [1] * (count - 1)
    while surplus > 0:
        movable = [i for i in range(count - 1) if holding[i] < most]
        mass, left = sum([portions[i] for i in movable]), surplus
        for i in movable:
            more = min(most - holding[i], max(1, left * portions[i] // mass), surplus)
            holding[i] = holding[i] + more
            surplus = surplus - more
    return np.array([most] + holding)


def uneven(key, amount, total, bound, lean):
    if amount == 2:
        one = jax.random.randint(key, (), max(1, total - bound), min(bound, total - 1) + 1)
        return jnp.stack([one, total - one])
    sizes = jnp.asarray(profile(amount, total, bound, lean), jnp.int32)
    couples = (amount - 1) // 2
    giver, sink = sizes[1:1 + 2 * couples:2], sizes[2:2 + 2 * couples:2]
    margin = jnp.minimum(giver - 1, bound - sink)
    passed = jax.random.randint(jax.random.fold_in(key, 1), (couples,), 0, 1 << 20) % (margin + 1)
    sizes = sizes.at[1:1 + 2 * couples:2].set(giver - passed).at[2:2 + 2 * couples:2].set(sink + passed)
    return sizes[jax.random.permutation(jax.random.fold_in(key, 2), amount)]


def bell_draw(own_key, shape, scale, reach, cuts=(), kind=jnp.bfloat16):
    gain = levels(own_key, shape, cuts, -0.22, 0.18) if cuts else 1.0
    drawn = jax.random.normal(own_key, shape, jnp.float32) * scale * gain
    return jnp.minimum(jnp.maximum(drawn, -reach), reach).astype(kind)


def setup_inputs(seed: int = 0) -> dict:
    seeds = jax.random.split(jax.random.key(seed), 19)
    tokens_in = bell_draw(seeds[0], (TOKENS, D), 1.0, 6.0, ((0, 8), (1, 4)))
    out_cot = bell_draw(seeds[1], (TOKENS, D), 1.0, 6.0, ((0, 8), (1, 4)))
    segments = jax.vmap(lambda own: jnp.searchsorted(jnp.cumsum(uneven(own, SEQ_LEN // 16, SEQ_LEN, SEQ_LEN // 2, 2)), jnp.arange(SEQ_LEN), side="right"))(jax.random.split(seeds[2], SEQUENCES)).reshape((SEQUENCES, SEQ_LEN)).astype(jnp.int32)
    norm_params = draw_norm_params(jax.random.fold_in(seeds[18], 71), 0)
    qkv_weight = bell_draw(seeds[4], (D, 3 * D), D ** -0.5, 0.21875, ((0, 4), (1, 2)), jnp.float32)
    proj_weight = bell_draw(seeds[5], (D, D), (D // 16) ** -0.5, 0.875, ((0, 2), (1, 4)), jnp.float32)
    up_weight = bell_draw(seeds[6], (D, FF), D ** -0.5, 0.21875, ((0, 4), (1, 2)), jnp.float32)
    down_weight = bell_draw(seeds[7], (FF, D), FF ** -0.5, 0.109375, ((0, 2), (1, 4)), jnp.float32)
    norm_first = bell_draw(seeds[8], (4, D), 3.0, 18.0, ((1, 4),), jnp.float32)
    norm_second = jnp.clip(jnp.exp(math.log(300.0) - 2.3025851 * jax.random.uniform(seeds[9], (4, D), jnp.float32) ** levels(seeds[9], (4, D), ((1, 4),), -0.2, 0.2)), 30.0, 300.0)
    qkv_first = bell_draw(seeds[10], (D, 3 * D), 3.0, 18.0, ((0, 4), (1, 2)), jnp.float32)
    qkv_second = jnp.clip(jnp.exp(math.log(300.0) - 2.3025851 * jax.random.uniform(seeds[11], (D, 3 * D), jnp.float32) ** levels(seeds[11], (D, 3 * D), ((0, 4), (1, 2)), -0.2, 0.2)), 30.0, 300.0)
    proj_first = bell_draw(seeds[12], (D, D), 3.0, 18.0, ((0, 2), (1, 4)), jnp.float32)
    proj_second = jnp.clip(jnp.exp(math.log(300.0) - 2.3025851 * jax.random.uniform(seeds[13], (D, D), jnp.float32) ** levels(seeds[13], (D, D), ((0, 2), (1, 4)), -0.2, 0.2)), 30.0, 300.0)
    up_first = bell_draw(seeds[14], (D, FF), 3.0, 18.0, ((0, 4), (1, 2)), jnp.float32)
    up_second = jnp.clip(jnp.exp(math.log(300.0) - 2.3025851 * jax.random.uniform(seeds[15], (D, FF), jnp.float32) ** levels(seeds[15], (D, FF), ((0, 4), (1, 2)), -0.2, 0.2)), 30.0, 300.0)
    down_first = bell_draw(seeds[16], (FF, D), 3.0, 18.0, ((0, 2), (1, 4)), jnp.float32)
    down_second = jnp.clip(jnp.exp(math.log(300.0) - 2.3025851 * jax.random.uniform(seeds[17], (FF, D), jnp.float32) ** levels(seeds[17], (FF, D), ((0, 2), (1, 4)), -0.2, 0.2)), 30.0, 300.0)
    return {"tokens_in": tokens_in, "out_cot": out_cot, "segments": segments, "norm_params": norm_params, "qkv_weight": qkv_weight, "proj_weight": proj_weight, "up_weight": up_weight, "down_weight": down_weight, "norm_first": norm_first, "norm_second": norm_second, "qkv_first": qkv_first, "qkv_second": qkv_second, "proj_first": proj_first, "proj_second": proj_second, "up_first": up_first, "up_second": up_second, "down_first": down_first, "down_second": down_second}


norm_eps = 1e-05
rotary_base = 10000.0
learn_rate = 0.01
beta_first = 0.9
beta_second = 0.95
adam_eps = 1e-08
decay_rate = 0.1
mask_fill = -1e+30
inv_sqrt_two = 0.7071067811865476
inv_sqrt_two_pi = 0.3989422804014327

def gelu_value(value):
    return 0.5 * value * (1.0 + lax.erf(value * inv_sqrt_two))

def gelu_slope(value):
    return 0.5 * (1.0 + lax.erf(value * inv_sqrt_two)) + value * inv_sqrt_two_pi * jnp.exp(-0.5 * value * value)

def positions_of(segs):
    length = segs.shape[-1]
    index = jnp.broadcast_to(jnp.arange(length, dtype=jnp.int32), segs.shape)
    starts = jnp.concatenate([jnp.ones(segs.shape[:-1] + (1,), bool), segs[..., 1:] != segs[..., :-1]], -1)
    first = lax.cummax(jnp.where(starts, index, 0).astype(jnp.int32), axis=segs.ndim - 1)
    return index - first

def rotary_tables(positions):
    half = ROT_DIM // 2
    freq = rotary_base ** (-2.0 * jnp.arange(half, dtype=jnp.float32) / ROT_DIM)
    angle = positions.astype(jnp.float32)[..., None] * freq
    return (jnp.cos(angle), jnp.sin(angle))

def rotate(tensor, cosine, sine):
    half = ROT_DIM // 2
    cos_part = cosine[..., None, :]
    sin_part = sine[..., None, :]
    front = tensor[..., :half]
    back = tensor[..., half:ROT_DIM]
    return jnp.concatenate([front * cos_part - back * sin_part, back * cos_part + front * sin_part, tensor[..., ROT_DIM:]], -1)

def rotate_back(grad, cosine, sine):
    half = ROT_DIM // 2
    cos_part = cosine[..., None, :]
    sin_part = sine[..., None, :]
    front = grad[..., :half]
    back = grad[..., half:ROT_DIM]
    return jnp.concatenate([front * cos_part + back * sin_part, back * cos_part - front * sin_part, grad[..., ROT_DIM:]], -1)

def masked_scores(query, keys, segment):
    length = segment.shape[0]
    scores = jnp.einsum('qhd,khd->hqk', query.astype(jnp.float32), keys.astype(jnp.float32)) / math.sqrt(HEAD_DIM)
    index = jnp.arange(length, dtype=jnp.int32)
    allowed = (segment[:, None] == segment[None, :]) & (index[None, :] <= index[:, None])
    return jnp.where(allowed[None], scores, mask_fill)

def attend(query, keys, values, segment):
    scores = masked_scores(query, keys, segment)
    total = lax.optimization_barrier(jnp.sum(jnp.exp(scores), -1, keepdims=True))
    logsum = jnp.log(total)
    weights = jnp.exp(scores - logsum).astype(jnp.bfloat16)
    mixed = jnp.einsum('hqk,khd->qhd', weights.astype(jnp.float32), values.astype(jnp.float32)).astype(jnp.bfloat16)
    return (mixed, logsum[..., 0])

def attend_back(query, keys, values, segment, logsum, mixed, grad_mixed):
    scores = masked_scores(query, keys, segment)
    probs = jnp.exp(scores - logsum[..., None])
    weights = probs.astype(jnp.bfloat16).astype(jnp.float32)
    grad_f = grad_mixed.astype(jnp.float32)
    value_grad = jnp.einsum('hqk,qhd->khd', weights, grad_f)
    prod_grad = jnp.einsum('qhd,khd->hqk', grad_f, values.astype(jnp.float32))
    delta = lax.optimization_barrier(jnp.sum(grad_f * mixed.astype(jnp.float32), -1)).T
    score_grad = (probs * (prod_grad - delta[..., None]) / math.sqrt(HEAD_DIM)).astype(jnp.bfloat16).astype(jnp.float32)
    query_grad = jnp.einsum('hqk,khd->qhd', score_grad, keys.astype(jnp.float32))
    key_grad = jnp.einsum('hqk,qhd->khd', score_grad, query.astype(jnp.float32))
    return (query_grad, key_grad, value_grad)

def dot32(left, right):
    return jnp.dot(left, right, preferred_element_type=jnp.float32)

def run_block(tokens, cotan, segs, gains, qkv16, proj16, up16, down16):
    count = tokens.shape[0]
    nseq = segs.shape[0]
    xfull = tokens.astype(jnp.float32)
    mean = lax.optimization_barrier(jnp.mean(xfull, -1, keepdims=True))
    spread = lax.optimization_barrier(jnp.mean(xfull * xfull, -1, keepdims=True)) - mean * mean
    rstd = lax.rsqrt(spread + norm_eps)
    normed = (xfull - mean) * rstd
    first_in = (normed * gains[0] + gains[1]).astype(jnp.bfloat16)
    second_in = (normed * gains[2] + gains[3]).astype(jnp.bfloat16)
    packed = dot32(first_in, qkv16).reshape(nseq, SEQ_LEN, HEADS, 3, HEAD_DIM)
    cosine, sine = rotary_tables(positions_of(segs))
    query = rotate(packed[..., 0, :], cosine, sine).astype(jnp.bfloat16)
    keys = rotate(packed[..., 1, :], cosine, sine).astype(jnp.bfloat16)
    values = packed[..., 2, :].astype(jnp.bfloat16)
    attended, logsum = lax.map(lambda item: attend(*item), (query, keys, values, segs))
    attended_flat = attended.reshape(count, D)
    hidden = dot32(second_in, up16)
    active = gelu_value(hidden).astype(jnp.bfloat16)
    output = (xfull + dot32(attended_flat, proj16) + dot32(active, down16)).astype(jnp.bfloat16)
    proj_grad = dot32(attended_flat.T, cotan)
    down_grad = dot32(active.T, cotan)
    attended_grad = dot32(cotan, proj16.T).astype(jnp.bfloat16)
    hidden_grad = (dot32(cotan, down16.T) * gelu_slope(hidden)).astype(jnp.bfloat16)
    grad_heads = attended_grad.reshape(nseq, SEQ_LEN, HEADS, HEAD_DIM)
    query_grad, key_grad, value_grad = lax.map(lambda item: attend_back(*item), (query, keys, values, segs, logsum, attended, grad_heads))
    query_grad = rotate_back(query_grad, cosine, sine)
    key_grad = rotate_back(key_grad, cosine, sine)
    packed_grad = jnp.stack([query_grad, key_grad, value_grad], 3).reshape(count, 3 * D).astype(jnp.bfloat16)
    qkv_grad = dot32(first_in.T, packed_grad)
    up_grad = dot32(second_in.T, hidden_grad)
    first_grad = dot32(packed_grad, qkv16.T)
    second_grad = dot32(hidden_grad, up16.T)
    norm_grad = jnp.stack([lax.optimization_barrier(jnp.sum(first_grad * normed, 0)), lax.optimization_barrier(jnp.sum(first_grad, 0)), lax.optimization_barrier(jnp.sum(second_grad * normed, 0)), lax.optimization_barrier(jnp.sum(second_grad, 0))], 0)
    combined = gains[0] * first_grad + gains[2] * second_grad
    input_grad = (cotan.astype(jnp.float32) + rstd * (combined - lax.optimization_barrier(jnp.mean(combined, -1, keepdims=True)) - normed * lax.optimization_barrier(jnp.mean(combined * normed, -1, keepdims=True)))).astype(jnp.bfloat16)
    return (output, input_grad, (norm_grad, qkv_grad, proj_grad, up_grad, down_grad))

def adam_update(weight, first, second, grad, decay):
    first_new = beta_first * first + (1.0 - beta_first) * grad
    second_new = beta_second * second + (1.0 - beta_second) * grad * grad
    first_hat = first_new / (1.0 - beta_first ** STEP)
    second_hat = second_new / (1.0 - beta_second ** STEP)
    weight_new = weight - learn_rate * (first_hat / (jnp.sqrt(second_hat) + adam_eps) + decay * weight)
    return (weight_new, first_new, second_new)

def reference(tokens_in, out_cot, segments, norm_params, qkv_weight, proj_weight, up_weight, down_weight, norm_first, norm_second, qkv_first, qkv_second, proj_first, proj_second, up_first, up_second, down_first, down_second):
    qkv16 = qkv_weight.astype(jnp.bfloat16)
    proj16 = proj_weight.astype(jnp.bfloat16)
    up16 = up_weight.astype(jnp.bfloat16)
    down16 = down_weight.astype(jnp.bfloat16)
    block_seqs = math.gcd(SEQUENCES, 8)
    blocks = SEQUENCES // block_seqs
    tok_blocks = tokens_in.reshape(blocks, block_seqs * SEQ_LEN, D)
    cot_blocks = out_cot.reshape(blocks, block_seqs * SEQ_LEN, D)
    seg_blocks = segments.reshape(blocks, block_seqs, SEQ_LEN)
    zeros = (jnp.zeros((4, D), jnp.float32), jnp.zeros((D, 3 * D), jnp.float32), jnp.zeros((D, D), jnp.float32), jnp.zeros((D, FF), jnp.float32), jnp.zeros((FF, D), jnp.float32))

    def scan_step(carry, item):
        output, input_grad, grads = run_block(item[0], item[1], item[2], norm_params, qkv16, proj16, up16, down16)
        carry = jax.tree.map(lambda total, part: total + part, carry, grads)
        return (carry, (output, input_grad))
    grads, outs = lax.scan(scan_step, zeros, (tok_blocks, cot_blocks, seg_blocks))
    output = outs[0].reshape(TOKENS, D)
    input_grad = outs[1].reshape(TOKENS, D)
    norm_grad, qkv_grad, proj_grad, up_grad, down_grad = grads
    norm_new, norm_first_new, norm_second_new = adam_update(norm_params, norm_first, norm_second, norm_grad, 0.0)
    qkv_new, qkv_first_new, qkv_second_new = adam_update(qkv_weight, qkv_first, qkv_second, qkv_grad, decay_rate)
    proj_new, proj_first_new, proj_second_new = adam_update(proj_weight, proj_first, proj_second, proj_grad, decay_rate)
    up_new, up_first_new, up_second_new = adam_update(up_weight, up_first, up_second, up_grad, decay_rate)
    down_new, down_first_new, down_second_new = adam_update(down_weight, down_first, down_second, down_grad, decay_rate)
    return (output, input_grad, norm_grad, qkv_grad, proj_grad, up_grad, down_grad, norm_new, qkv_new, proj_new, up_new, down_new, norm_first_new, norm_second_new, qkv_first_new, qkv_second_new, proj_first_new, proj_second_new, up_first_new, up_second_new, down_first_new, down_second_new)
```

```python
import math

import jax
import jax.numpy as jnp
from jax import lax
from jax.sharding import PartitionSpec as P

D = 768
HEAD_DIM = 64
ROT_DIM = 16
SEQ_LEN = 512
STEP = 3


norm_eps = 1e-05
rotary_base = 10000.0
learn_rate = 0.01
beta_first = 0.9
beta_second = 0.95
adam_eps = 1e-08
decay_rate = 0.1
mask_fill = -1e30
inv_sqrt_two = 0.7071067811865476
inv_sqrt_two_pi = 0.3989422804014327


def gelu_value(value):
    return 0.5 * value * (1.0 + lax.erf(value * inv_sqrt_two))


def gelu_slope(value):
    return 0.5 * (1.0 + lax.erf(value * inv_sqrt_two)) + value * inv_sqrt_two_pi * jnp.exp(
        -0.5 * value * value
    )


def positions_of(segs):
    length = segs.shape[-1]
    index = jnp.broadcast_to(jnp.arange(length, dtype=jnp.int32), segs.shape)
    starts = jnp.concatenate(
        [jnp.ones(segs.shape[:-1] + (1,), bool), segs[..., 1:] != segs[..., :-1]], -1
    )
    first = lax.cummax(jnp.where(starts, index, 0), axis=segs.ndim - 1)
    return index - first


def rotary_tables(positions):
    half = ROT_DIM // 2
    freq = rotary_base ** (-2.0 * jnp.arange(half, dtype=jnp.float32) / ROT_DIM)
    angle = positions.astype(jnp.float32)[..., None] * freq
    return (jnp.cos(angle), jnp.sin(angle))


def rotate(tensor, cosine, sine):
    half = ROT_DIM // 2
    cos_part = cosine[..., None, :]
    sin_part = sine[..., None, :]
    front = tensor[..., :half]
    back = tensor[..., half:ROT_DIM]
    return jnp.concatenate(
        [
            front * cos_part - back * sin_part,
            back * cos_part + front * sin_part,
            tensor[..., ROT_DIM:],
        ],
        -1,
    )


def rotate_back(grad, cosine, sine):
    half = ROT_DIM // 2
    cos_part = cosine[..., None, :]
    sin_part = sine[..., None, :]
    front = grad[..., :half]
    back = grad[..., half:ROT_DIM]
    return jnp.concatenate(
        [
            front * cos_part + back * sin_part,
            back * cos_part - front * sin_part,
            grad[..., ROT_DIM:],
        ],
        -1,
    )


def masked_scores(query, keys, segment):
    length = segment.shape[0]
    scores = jnp.einsum(
        "qhd,khd->hqk", query, keys, preferred_element_type=jnp.float32
    ) / math.sqrt(HEAD_DIM)
    index = jnp.arange(length, dtype=jnp.int32)
    allowed = (segment[:, None] == segment[None, :]) & (index[None, :] <= index[:, None])
    return jnp.where(allowed[None], scores, mask_fill)


def attend(query, keys, values, segment):
    scores = masked_scores(query, keys, segment)
    total = jnp.sum(jnp.exp(scores), -1, keepdims=True)
    logsum = jnp.log(total)
    weights = jnp.exp(scores - logsum).astype(jnp.bfloat16)
    mixed = jnp.einsum("hqk,khd->qhd", weights, values, preferred_element_type=jnp.float32).astype(
        jnp.bfloat16
    )
    return (mixed, logsum[..., 0])


def attend_back(query, keys, values, segment, logsum, mixed, grad_mixed):
    scores = masked_scores(query, keys, segment)
    probs = jnp.exp(scores - logsum[..., None])
    weights = probs.astype(jnp.bfloat16)
    value_grad = jnp.einsum("hqk,qhd->khd", weights, grad_mixed, preferred_element_type=jnp.float32)
    prod_grad = jnp.einsum("qhd,khd->hqk", grad_mixed, values, preferred_element_type=jnp.float32)
    delta = jnp.sum(grad_mixed.astype(jnp.float32) * mixed.astype(jnp.float32), -1).T
    score_grad = (probs * (prod_grad - delta[..., None]) / math.sqrt(HEAD_DIM)).astype(jnp.bfloat16)
    query_grad = jnp.einsum("hqk,khd->qhd", score_grad, keys, preferred_element_type=jnp.float32)
    key_grad = jnp.einsum("hqk,qhd->khd", score_grad, query, preferred_element_type=jnp.float32)
    return (query_grad, key_grad, value_grad)


def dot32(left, right):
    return jnp.dot(left, right, preferred_element_type=jnp.float32)


def dot_rows(left, right):
    return lax.dot_general(
        left, right, (((0,), (0,)), ((), ())), preferred_element_type=jnp.float32
    )


def dot_cols(left, right):
    return lax.dot_general(
        left, right, (((1,), (1,)), ((), ())), preferred_element_type=jnp.float32
    )


def adam_update(weight, first, second, grad, decay):
    first_new = beta_first * first + (1.0 - beta_first) * grad
    second_new = beta_second * second + (1.0 - beta_second) * grad * grad
    first_hat = first_new / (1.0 - beta_first**STEP)
    second_hat = second_new / (1.0 - beta_second**STEP)
    weight_new = weight - learn_rate * (
        first_hat / (jnp.sqrt(second_hat) + adam_eps) + decay * weight
    )
    return (weight_new, first_new, second_new)


def gather_weight(piece):
    rows = piece.shape[0] // lax.axis_size("dp")
    own = lax.dynamic_slice_in_dim(piece, lax.axis_index("dp") * rows, rows, 0)
    return lax.all_gather(own, ("row", "dp"), axis=0, tiled=True)


def reduce_weights(grads):
    whole = jnp.concatenate([grad.astype(jnp.bfloat16) for grad in grads], 1)
    part = lax.psum_scatter(whole, ("row", "dp"), scatter_dimension=0, tiled=True)
    sums, start = [], 0
    for grad in grads:
        piece = part[:, start : start + grad.shape[1]]
        sums.append(lax.all_gather(piece, "dp", axis=0, tiled=True).astype(jnp.float32))
        start += grad.shape[1]
    return sums


def on_device(
    tokens_in,
    out_cot,
    segments,
    norm_params,
    qkv_weight,
    proj_weight,
    up_weight,
    down_weight,
    norm_first,
    norm_second,
    qkv_first,
    qkv_second,
    proj_first,
    proj_second,
    up_first,
    up_second,
    down_first,
    down_second,
):
    row_count = lax.axis_size("row")
    row_index = lax.axis_index("row")
    col_count = lax.axis_size("col")
    col_index = lax.axis_index("col")
    local_count, local_width = tokens_in.shape
    heads_here = qkv_weight.shape[1] // (3 * HEAD_DIM)
    seq_count = segments.shape[0] // row_count
    group_count = local_count * col_count
    share = group_count // row_count
    width = local_width * row_count
    bf16 = jnp.bfloat16

    def to_tokens(rows):
        blocks = rows.reshape(row_count, share, local_width)
        blocks = lax.all_to_all(blocks, "row", 0, 0, tiled=True)
        return jnp.moveaxis(blocks, 0, 1).reshape(share, width)

    x16 = to_tokens(lax.all_gather(tokens_in, "col", axis=0, tiled=True))
    cot16 = to_tokens(lax.all_gather(out_cot, "col", axis=0, tiled=True))
    norm_full = lax.all_gather(norm_params, "row", axis=1, tiled=True)
    pieces = (qkv_weight, up_weight, proj_weight.T, down_weight.T)
    all16 = gather_weight(jnp.concatenate([piece.astype(bf16) for piece in pieces], 1))
    first_cut = qkv_weight.shape[1]
    second_cut = first_cut + up_weight.shape[1]
    qkv16 = all16[:, :first_cut]
    up16 = all16[:, first_cut:second_cut]
    out16 = all16[:, second_cut:]

    xfull = x16.astype(jnp.float32)
    mean = jnp.sum(xfull, 1, keepdims=True) / D
    spread = jnp.sum(xfull * xfull, 1, keepdims=True) / D - mean * mean
    rstd = lax.rsqrt(spread + norm_eps)
    normed = (xfull - mean) * rstd
    first_in = (normed * norm_full[0] + norm_full[1]).astype(bf16)
    second_in = (normed * norm_full[2] + norm_full[3]).astype(bf16)
    qkv_own = dot32(first_in, qkv16)
    hidden_here = dot32(second_in, up16)

    width_qkv = qkv16.shape[1]
    seg_own = lax.dynamic_slice_in_dim(segments, row_index * seq_count, seq_count, 0)
    cosine, sine = rotary_tables(positions_of(seg_own))
    packed = qkv_own.reshape(seq_count, SEQ_LEN, heads_here, 3, HEAD_DIM)
    query = rotate(packed[..., 0, :], cosine, sine).astype(bf16)
    keys = rotate(packed[..., 1, :], cosine, sine).astype(bf16)
    values = packed[..., 2, :].astype(bf16)
    attended, logsum = lax.map(lambda item: attend(*item), (query, keys, values, seg_own))
    attn_width = heads_here * HEAD_DIM
    attn_flat = attended.reshape(share, attn_width)
    active = gelu_value(hidden_here).astype(bf16)
    act_cat = jnp.concatenate([attn_flat, active], 1)
    out_part = dot_cols(act_cat, out16)
    out_grad = dot_rows(cot16, act_cat)
    act_grad = dot32(cot16, out16)
    attended_grad = act_grad[:, :attn_width].astype(bf16)
    hidden_grad = (act_grad[:, attn_width:] * gelu_slope(hidden_here)).astype(bf16)
    up_grad = dot_rows(second_in, hidden_grad)
    grad_heads = attended_grad.reshape(seq_count, SEQ_LEN, heads_here, HEAD_DIM)
    query_grad, key_grad, value_grad = lax.map(
        lambda item: attend_back(*item),
        (query, keys, values, seg_own, logsum, attended, grad_heads),
    )
    query_grad = rotate_back(query_grad, cosine, sine)
    key_grad = rotate_back(key_grad, cosine, sine)
    packed_grad = (
        jnp.stack([query_grad, key_grad, value_grad], 3).reshape(share, width_qkv).astype(bf16)
    )
    qkv_grad = dot_rows(first_in, packed_grad)
    qkv_grad, up_grad, out_grad = reduce_weights((qkv_grad, up_grad, out_grad))
    first_grad = dot_cols(packed_grad, qkv16)
    second_grad = dot_cols(hidden_grad, up16)
    norm_part = jnp.stack(
        [
            jnp.sum(first_grad * normed, 0),
            jnp.sum(first_grad, 0),
            jnp.sum(second_grad * normed, 0),
            jnp.sum(second_grad, 0),
        ],
        0,
    )
    combined = norm_full[0] * first_grad + norm_full[2] * second_grad
    back_first = jnp.sum(combined, 1, keepdims=True) / D
    back_second = jnp.sum(combined * normed, 1, keepdims=True) / D
    grad_part = rstd * (combined - back_first - normed * back_second)

    def to_features(part):
        blocks = part.astype(bf16).reshape(share, row_count, local_width)
        blocks = lax.all_to_all(jnp.moveaxis(blocks, 1, 0), "row", 0, 0, tiled=True)
        parts = blocks.reshape(col_count, local_count, local_width)
        total = lax.dynamic_index_in_dim(parts, col_index, 0, keepdims=False).astype(jnp.float32)
        for step in range(1, col_count):
            peer = lax.rem(col_index + step, col_count)
            sent = lax.dynamic_index_in_dim(parts, peer, 0, keepdims=False)
            ring = [(i, (i + step) % col_count) for i in range(col_count)]
            total = total + lax.ppermute(sent, "col", ring).astype(jnp.float32)
        return total

    output = (tokens_in.astype(jnp.float32) + to_features(out_part)).astype(bf16)
    input_grad = (out_cot.astype(jnp.float32) + to_features(grad_part)).astype(bf16)
    norm_grad = lax.dynamic_slice_in_dim(
        lax.psum(norm_part, ("dp", "row", "col")), row_index * local_width, local_width, 1
    )
    proj_grad = out_grad[:, :attn_width].T
    down_grad = out_grad[:, attn_width:].T
    norm_new, norm_first_new, norm_second_new = adam_update(
        norm_params, norm_first, norm_second, norm_grad, 0.0
    )
    qkv_new, qkv_first_new, qkv_second_new = adam_update(
        qkv_weight, qkv_first, qkv_second, qkv_grad, decay_rate
    )
    proj_new, proj_first_new, proj_second_new = adam_update(
        proj_weight, proj_first, proj_second, proj_grad, decay_rate
    )
    up_new, up_first_new, up_second_new = adam_update(
        up_weight, up_first, up_second, up_grad, decay_rate
    )
    down_new, down_first_new, down_second_new = adam_update(
        down_weight, down_first, down_second, down_grad, decay_rate
    )
    return (
        output,
        input_grad,
        norm_grad,
        qkv_grad,
        proj_grad,
        up_grad,
        down_grad,
        norm_new,
        qkv_new,
        proj_new,
        up_new,
        down_new,
        norm_first_new,
        norm_second_new,
        qkv_first_new,
        qkv_second_new,
        proj_first_new,
        proj_second_new,
        up_first_new,
        up_second_new,
        down_first_new,
        down_second_new,
    )


def solution(mesh):
    placed = (
        P(("dp", "col"), "row"),
        P(("dp", "col"), "row"),
        P("dp", None),
        P(None, "row"),
        P("row", "col"),
        P("col", "row"),
        P("row", "col"),
        P("col", "row"),
        P(None, "row"),
        P(None, "row"),
        P("row", "col"),
        P("row", "col"),
        P("col", "row"),
        P("col", "row"),
        P("row", "col"),
        P("row", "col"),
        P("col", "row"),
        P("col", "row"),
    )
    return jax.shard_map(
        on_device,
        mesh=mesh,
        in_specs=placed,
        out_specs=(
            P(("dp", "col"), "row"),
            P(("dp", "col"), "row"),
            P(None, "row"),
            P("row", "col"),
            P("col", "row"),
            P("row", "col"),
            P("col", "row"),
            P(None, "row"),
            P("row", "col"),
            P("col", "row"),
            P("row", "col"),
            P("col", "row"),
            P(None, "row"),
            P(None, "row"),
            P("row", "col"),
            P("row", "col"),
            P("col", "row"),
            P("col", "row"),
            P("row", "col"),
            P("row", "col"),
            P("col", "row"),
            P("col", "row"),
        ),
        check_vma=False,
    )
```
